512 devices in a mesh: grp: 128 (over y, x, z_hi, core), qtr: 4 (over z_lo).
Axes of the slice: x: 4, y: 8, z: 8 (z_hi: 2, z_lo: 4; z = z_hi * 4 + z_lo), core: 2. Of those that a mesh axis runs over, the one named last changes fastest.
Arguments:
- vectors: float32 [131072, 512], P(('grp', 'qtr')), may hold values from -6 to 6
- previous: float32 [131072, 512], P(('grp', 'qtr')), may hold values from -6 to 6
- diag_tiles: bfloat16 [1024, 4, 128, 128], P(('grp', 'qtr')), may hold values from -0.125 to 0.125
- diag_cols: int32 [1024, 4], P(('grp', 'qtr')), may hold values from 0 to 7, all different within a row
- diag_mask: int32 [1024, 4], P(('grp', 'qtr')), may hold values 0 or 1
- off_tiles: bfloat16 [3, 1024, 4, 128, 128], P(None, ('grp', 'qtr')), may hold values from -0.125 to 0.125
- off_rows: int32 [3, 1024, 4], P(None, ('grp', 'qtr')), may hold values from 0 to 7, all different within a row
- off_mask: int32 [3, 1024, 4], P(None, ('grp', 'qtr')), may hold values 0 or 1
Outputs:
- chebyshev: float32 [131072, 512], P(('grp', 'qtr'))
The draws below stay inside these ranges and needn't reach their ends.
Inputs may be any that keep to these rules, and one draw needn't show every extreme that they name: `diag_cols`: each row names 4 different tile columns of the group. `off_rows`: each row names 4 different tile rows of the group.
All inputs are finite; a program needn't handle non-finite values. No bound on the sum of `diag_mask` or of `off_mask` on one device may be relied on, other than what follows from the above.
Results may differ from the reference program's by a relative error of at most 0.002.
Values may be sent and summed in bfloat16 or wider, within the bound.
No kernel may reach another device: no remote copies, remote signals or barrier semaphores. Data moves between devices by JAX's collectives and lax.ppermute only.
A program may use at most 64 MiB of HBM per device.

```python
import jax
import jax.numpy as jnp
from jax import lax

K = 512
TILE = 128
TR_DEV = 2
GROUP_TILES = 8
SLOTS = 4
ROWS = 131072
N_GRP = 128
N_QTR = 4


def with_ends(drawn, stream_key, least, high):
    spot = [jax.random.randint(jax.random.fold_in(stream_key, axis), (), 0, length) for axis, length in enumerate(drawn.shape)]
    widest = drawn.shape.index(max(drawn.shape))
    next_to = spot[:widest] + [(spot[widest] + 1) % drawn.shape[widest]] + spot[widest + 1:]
    return drawn.at[tuple(spot)].set(least).at[tuple(next_to)].set(high)


def level_of(rng, shape, split, least, largest):
    factor_of = 1.0
    for dim, blocks in split:
        steps = jax.random.uniform(jax.random.fold_in(jax.random.fold_in(rng, 6), dim), (blocks,), jnp.float32, least / len(split), largest / len(split))
        factor_of = factor_of * jnp.repeat(jnp.exp(steps), shape[dim] // blocks).reshape((-1,) + (1,) * (len(shape) - 1 - dim))
    return factor_of


def different_ones(rng, rows, amount, top, lift):
    ranking = jax.random.permutation(jax.random.fold_in(rng, 1), amount)
    favour = ranking
    for power in range(3):
        favour = favour * favour // amount
    favour = favour * lift // amount
    tickets = jax.random.randint(jax.random.fold_in(rng, 2), (rows, amount), 0, 4096) + favour
    holders = jax.random.permutation(jax.random.fold_in(rng, 3), rows)[jnp.arange(amount) % rows]
    tickets = jnp.where(jnp.arange(rows)[:, None] == holders[None, :], 1 << 14, tickets)
    priority = tickets * amount + jnp.arange(amount)
    return lax.top_k(priority.astype(jnp.int32), top)[1].astype(jnp.int32)


def bell_draw(own_key, dims, deviation, limit, shards=(), kind=jnp.bfloat16):
    drawn = jax.random.normal(own_key, dims, jnp.float32) * deviation
    if len(shards) > 0:
        drawn = level_of(own_key, dims, shards, -0.22, 0.18) * drawn
    return jnp.clip(drawn, min=-limit, max=limit).astype(kind)


def setup_inputs(seed: int = 0) -> dict:
    seeds = jax.random.split(jax.random.key(seed), 9)
    vectors = bell_draw(seeds[0], (ROWS, K), 1.0, 6.0, ((0, 512),), jnp.float32)
    previous = bell_draw(seeds[1], (ROWS, K), 1.0, 6.0, ((0, 512),), jnp.float32)
    diag_tiles = bell_draw(seeds[2], (N_GRP * GROUP_TILES, SLOTS, TILE, TILE), (4 * SLOTS * TILE) ** -0.5, 0.125, ((0, 512),))
    diag_cols = different_ones(seeds[3], (N_GRP * GROUP_TILES), GROUP_TILES, SLOTS, 0)
    diag_mask = with_ends((jax.random.randint(seeds[4], (N_GRP * GROUP_TILES, SLOTS), 0, 2) < 1).astype(jnp.int32), jax.random.fold_in(seeds[4], 1), 0, 1)
    off_tiles = bell_draw(seeds[5], (3, N_GRP * GROUP_TILES, SLOTS, TILE, TILE), (4 * SLOTS * TILE) ** -0.5, 0.125, ((1, 512),))
    off_rows = different_ones(seeds[6], 3 * (N_GRP * GROUP_TILES), GROUP_TILES, SLOTS, 0).reshape((3, N_GRP * GROUP_TILES, SLOTS))
    off_mask = with_ends((jax.random.randint(seeds[7], (3, N_GRP * GROUP_TILES, SLOTS), 0, 2) < 1).astype(jnp.int32), jax.random.fold_in(seeds[7], 1), 0, 1)
    return dict(vectors=vectors, previous=previous, diag_tiles=diag_tiles, diag_cols=diag_cols, diag_mask=diag_mask, off_tiles=off_tiles, off_rows=off_rows, off_mask=off_mask)


cheb_center = 0.25
cheb_half = 2.0


def reference(vectors, previous, diag_tiles, diag_cols, diag_mask, off_tiles, off_rows, off_mask):
    group_tiles = TR_DEV * N_QTR
    levels = N_GRP.bit_length() - 1
    bit_list = [0, levels // 2, levels - 1]
    rounded = lax.optimization_barrier(vectors.astype(jnp.bfloat16))
    vec_full = rounded.astype(jnp.float32).reshape(N_GRP, group_tiles, TILE, K)
    diag_shaped = diag_tiles.reshape(N_GRP, group_tiles, SLOTS, TILE, TILE)
    diag_flags = diag_mask.reshape(N_GRP, group_tiles, SLOTS)
    diag_index = diag_cols.reshape(N_GRP, group_tiles, SLOTS).astype(jnp.int32)
    off_shaped = off_tiles.reshape(3, N_GRP, group_tiles, SLOTS, TILE, TILE)
    off_flags = off_mask.reshape(3, N_GRP, group_tiles, SLOTS)
    off_index = off_rows.reshape(3, N_GRP, group_tiles, SLOTS).astype(jnp.int32)
    highest = lax.Precision.HIGHEST

    def live_tiles(tile_set, flags):
        return tile_set.astype(jnp.float32) * flags[..., None, None].astype(jnp.float32)

    def one_group(index):
        own_vecs = vec_full[index]
        tile_set = live_tiles(diag_shaped[index], diag_flags[index])
        col_set = diag_index[index]
        result = jnp.einsum('tsab,tsbk->tak', tile_set, own_vecs[col_set], precision=highest)
        result = result.at[col_set].add(jnp.einsum('tsab,tak->tsbk', tile_set, own_vecs, precision=highest))
        for partner in range(3):
            other = jnp.bitwise_xor(index, jnp.int32(1 << bit_list[partner])).astype(jnp.int32)
            other_vecs = vec_full[other]
            mine = live_tiles(off_shaped[partner, index], off_flags[partner, index])
            mine_rows = off_index[partner, index]
            result = result.at[mine_rows].add(jnp.einsum('csab,cbk->csak', mine, other_vecs, precision=highest))
            theirs = live_tiles(off_shaped[partner, other], off_flags[partner, other])
            their_rows = off_index[partner, other]
            result = result + jnp.einsum('csab,csak->cbk', theirs, other_vecs[their_rows], precision=highest)
        return result

    applied = lax.map(one_group, jnp.arange(N_GRP, dtype=jnp.int32)).reshape(N_GRP * group_tiles * TILE, K)
    return (2.0 / cheb_half) * (applied - cheb_center * vectors) - previous
```

```python
import jax
import jax.numpy as jnp
from jax import lax
from jax.experimental import pallas as pl
from jax.experimental.pallas import tpu as pltpu
from jax.sharding import PartitionSpec as P

cheb_center = 0.25
cheb_half = 2.0


def swap(block, axis, mask):
    count = lax.axis_size(axis)
    return lax.ppermute(block, axis, [(i, i ^ mask) for i in range(count)])


def live(tile, flag):
    return (tile.astype(jnp.float32) * flag.astype(jnp.float32)).astype(jnp.bfloat16)


def dot_plain(a, b):
    return lax.dot_general(a, b, (((1,), (0,)), ((), ())), preferred_element_type=jnp.float32)


def dot_flipped(a, b):
    return lax.dot_general(a, b, (((0,), (0,)), ((), ())), preferred_element_type=jnp.float32)


def scatter_kernel(
    diag_cols, diag_mask, off_rows, off_mask, diag_tiles, off_tiles, own, arr0, arr1, arr2,
    keep, out1, out2, out3, acc,
):
    strips, slots, size, _ = diag_tiles.shape
    shift = strips * lax.axis_index("qtr")
    acc[...] = jnp.zeros_like(acc)
    arrivals = (arr0, arr1, arr2)
    for strip in range(strips):
        rows = pl.ds(strip * size, size)
        for slot in range(slots):
            place = pl.multiple_of((diag_cols[strip, slot] ^ shift) * size, size)
            tile = live(diag_tiles[strip, slot], diag_mask[strip, slot])
            acc[pl.ds(place, size), :] += dot_flipped(tile, own[rows, :])
        for partner in range(3):
            for slot in range(slots):
                place = pl.multiple_of((off_rows[partner, strip, slot] ^ shift) * size, size)
                tile = live(off_tiles[partner, strip, slot], off_mask[partner, strip, slot])
                acc[pl.ds(place, size), :] += dot_plain(tile, arrivals[partner][rows, :])
    span = strips * size
    keep[...] = acc[0:span, :]
    for part, out in enumerate((out1, out2, out3)):
        out[...] = acc[(part + 1) * span:(part + 2) * span, :].astype(jnp.bfloat16)


def fetch(parts, gathered, sems):
    span = parts[0].shape[0]
    copies = [
        pltpu.make_async_copy(part, gathered.at[pl.ds(i * span, span), :], sems.at[i])
        for i, part in enumerate(parts)
    ]
    for copy in copies:
        copy.start()
    for copy in copies:
        copy.wait()


def partner_products(partner, out, off_rows, off_mask, off_tiles, gathered, shift):
    strips, slots, size, _ = off_tiles.shape[1:]
    for strip in range(strips):
        total = None
        for slot in range(slots):
            place = pl.multiple_of((off_rows[partner, strip, slot] ^ shift) * size, size)
            tile = live(off_tiles[partner, strip, slot], off_mask[partner, strip, slot])
            term = dot_flipped(tile, gathered[pl.ds(place, size), :])
            total = term if total is None else total + term
        out[strip * size:(strip + 1) * size, :] = total.astype(out.dtype)


def far_kernel(off_rows, off_mask, off_tiles, part0, part1, part2, part3, out2, gathered, sems):
    shift = off_tiles.shape[1] * lax.axis_index("qtr")
    fetch((part0, part1, part2, part3), gathered, sems)
    partner_products(2, out2, off_rows, off_mask, off_tiles, gathered, shift)


def near_kernel(
    diag_cols, diag_mask, off_rows, off_mask, diag_tiles, off_tiles, part0, part1, part2, part3,
    keep, vectors, previous, out0, out1, base, gathered, sems,
):
    strips, slots, size, _ = diag_tiles.shape
    shift = strips * lax.axis_index("qtr")
    fetch((part0, part1, part2, part3), gathered, sems)
    partner_products(1, out1, off_rows, off_mask, off_tiles, gathered, shift)
    partner_products(0, out0, off_rows, off_mask, off_tiles, gathered, shift)
    for strip in range(strips):
        rows = pl.ds(strip * size, size)
        total = keep[rows, :]
        for slot in range(slots):
            place = pl.multiple_of((diag_cols[strip, slot] ^ shift) * size, size)
            tile = live(diag_tiles[strip, slot], diag_mask[strip, slot])
            total = total + dot_plain(tile, gathered[pl.ds(place, size), :])
        base[rows, :] = 2.0 / cheb_half * (total - cheb_center * vectors[rows, :]) - previous[rows, :]


smem = pl.BlockSpec(memory_space=pltpu.SMEM)
vmem = pl.BlockSpec(memory_space=pltpu.VMEM)
anywhere = pl.BlockSpec(memory_space=pl.ANY)


def on_device(vectors, previous, diag_tiles, diag_cols, diag_mask, off_tiles, off_rows, off_mask):
    rows, width = vectors.shape
    quarters = lax.axis_size("qtr")
    levels = lax.axis_size("grp").bit_length() - 1
    bits = [1 << 0, 1 << levels // 2, 1 << levels - 1]
    half = jax.ShapeDtypeStruct((rows, width), jnp.bfloat16)
    full = jax.ShapeDtypeStruct((rows, width), jnp.float32)
    group_half = pltpu.VMEM((quarters * rows, width), jnp.bfloat16)
    group_full = pltpu.VMEM((quarters * rows, width), jnp.float32)
    sems = pltpu.SemaphoreType.DMA((quarters,))

    own = vectors.astype(jnp.bfloat16)
    part2 = swap(own, "qtr", 2)
    arr2 = swap(own, "grp", bits[2])
    part1 = swap(own, "qtr", 1)
    arr1 = swap(own, "grp", bits[1])
    arr0 = swap(own, "grp", bits[0])
    part3 = swap(part2, "qtr", 1)

    keep, send1, send2, send3 = pl.pallas_call(
        scatter_kernel,
        in_specs=[smem] * 4 + [vmem] * 6,
        out_specs=[vmem] * 4,
        out_shape=[full, half, half, half],
        scratch_shapes=[group_full],
        name="scatter_terms",
    )(diag_cols, diag_mask, off_rows, off_mask, diag_tiles, off_tiles, own, arr0, arr1, arr2)
    got3 = swap(send3, "qtr", 3)
    got2 = swap(send2, "qtr", 2)
    got1 = swap(send1, "qtr", 1)

    away2 = pl.pallas_call(
        far_kernel,
        in_specs=[smem] * 2 + [vmem] + [anywhere] * 4,
        out_specs=vmem,
        out_shape=half,
        scratch_shapes=[group_half, sems],
        name="far_terms",
    )(off_rows, off_mask, off_tiles, own, part1, part2, part3)
    back2 = swap(away2, "grp", bits[2])
    away0, away1, base = pl.pallas_call(
        near_kernel,
        in_specs=[smem] * 4 + [vmem] * 2 + [anywhere] * 4 + [vmem] * 3,
        out_specs=[vmem] * 3,
        out_shape=[half, half, full],
        scratch_shapes=[group_half, sems],
        name="near_terms",
    )(
        diag_cols, diag_mask, off_rows, off_mask, diag_tiles, off_tiles, own, part1, part2, part3,
        keep, vectors, previous,
    )
    back1 = swap(away1, "grp", bits[1])
    back0 = swap(away0, "grp", bits[0])

    total = base
    for term in (back0, back1, got1, got3, got2, back2):
        total = total + 2.0 / cheb_half * term.astype(jnp.float32)
    return total


def solution(mesh):
    spread = P(("grp", "qtr"))
    spread_off = P(None, ("grp", "qtr"))
    in_specs = (spread,) * 5 + (spread_off,) * 3
    return jax.shard_map(
        on_device, mesh=mesh, in_specs=in_specs, out_specs=spread, check_vma=False
    )
```

```python
import jax
import jax.numpy as jnp
from jax import lax
from jax.experimental import pallas as pl
from jax.experimental.pallas import tpu as pltpu
from jax.sharding import PartitionSpec as P


cheb_center = 0.25
cheb_half = 2.0


def swap(block, axis, mask):
    count = lax.axis_size(axis)
    return lax.ppermute(block, axis, [(i, i ^ mask) for i in range(count)])


def live(tile, flag):
    return (tile.astype(jnp.float32) * flag.astype(jnp.float32)).astype(jnp.bfloat16)


def dot_plain(a, b):
    return lax.dot_general(a, b, (((1,), (0,)), ((), ())), preferred_element_type=jnp.float32)


def dot_flipped(a, b):
    return lax.dot_general(a, b, (((0,), (0,)), ((), ())), preferred_element_type=jnp.float32)


def spread_add(acc, tiles, flags, places, flipped, block, shift):
    slots, size, _ = tiles.shape
    for slot in range(slots):
        place = pl.multiple_of((places(slot) ^ shift) * size, size)
        tile = live(tiles[slot], flags(slot))
        product = dot_flipped(tile, block) if flipped else dot_plain(tile, block)
        acc[pl.ds(place, size), :] += product


def scatter_kernel(
    diag_cols, diag_mask, off_rows, off_mask, off_tiles, own, arr0, arr1, arr2, diag_stored,
    keep, out1, out2, out3, acc, diag_tiles, sem,
):
    load = pltpu.make_async_copy(diag_stored, diag_tiles, sem)
    load.start()
    strips, _, size, _ = diag_tiles.shape
    shift = strips * lax.axis_index("qtr")
    acc[...] = jnp.zeros_like(acc)
    for partner, arrived in enumerate((arr0, arr1, arr2)):
        for strip in range(strips):
            rows = pl.ds(strip * size, size)
            spread_add(
                acc, off_tiles.at[partner, strip], lambda i: off_mask[partner, strip, i],
                lambda i: off_rows[partner, strip, i], False, arrived[rows, :], shift,
            )
    load.wait()
    for strip in range(strips):
        rows = pl.ds(strip * size, size)
        spread_add(
            acc, diag_tiles.at[strip], lambda i: diag_mask[strip, i], lambda i: diag_cols[strip, i],
            True, own[rows, :], shift,
        )
    span = strips * size
    keep[...] = acc[0:span, :]
    for part, out in enumerate((out1, out2, out3)):
        out[...] = acc[(part + 1) * span:(part + 2) * span, :].astype(jnp.bfloat16)


def collect(parts, gathered):
    span = parts[0].shape[0]
    for i, part in enumerate(parts):
        gathered[i * span:(i + 1) * span, :] = part[...]


def partner_kernel(off_rows, off_mask, off_tiles, part0, part1, part2, part3, out0, out1, out2, gathered):
    strips, slots, size, _ = off_tiles.shape[1:]
    shift = strips * lax.axis_index("qtr")
    collect((part0, part1, part2, part3), gathered)
    for partner, out in ((2, out2), (1, out1), (0, out0)):
        for strip in range(strips):
            total = None
            for slot in range(slots):
                place = pl.multiple_of((off_rows[partner, strip, slot] ^ shift) * size, size)
                tile = live(off_tiles[partner, strip, slot], off_mask[partner, strip, slot])
                term = dot_flipped(tile, gathered[pl.ds(place, size), :])
                total = term if total is None else total + term
            out[strip * size:(strip + 1) * size, :] = total.astype(out.dtype)


def base_kernel(
    diag_cols, diag_mask, diag_tiles, part0, part1, part2, part3, keep, vectors, previous, base, gathered,
):
    strips, slots, size, _ = diag_tiles.shape
    shift = strips * lax.axis_index("qtr")
    collect((part0, part1, part2, part3), gathered)
    for strip in range(strips):
        rows = pl.ds(strip * size, size)
        total = keep[rows, :]
        for slot in range(slots):
            place = pl.multiple_of((diag_cols[strip, slot] ^ shift) * size, size)
            tile = live(diag_tiles[strip, slot], diag_mask[strip, slot])
            total = total + dot_plain(tile, gathered[pl.ds(place, size), :])
        base[rows, :] = 2.0 / cheb_half * (total - cheb_center * vectors[rows, :]) - previous[rows, :]


smem = pl.BlockSpec(memory_space=pltpu.SMEM)
vmem = pl.BlockSpec(memory_space=pltpu.VMEM)
anywhere = pl.BlockSpec(memory_space=pl.ANY)


def near(x):
    return pltpu.with_memory_space_constraint(x, pltpu.VMEM)


def far(x):
    return pltpu.with_memory_space_constraint(x, pltpu.HBM)


def call(kernel, scalars, arrays, outs, scratch, stored=()):
    return pl.pallas_call(
        kernel,
        in_specs=[smem] * len(scalars) + [vmem] * len(arrays) + [anywhere] * len(stored),
        out_specs=[vmem] * len(outs),
        out_shape=[pltpu.VMEM(shape, dtype) for shape, dtype in outs],
        scratch_shapes=scratch,
        compiler_params=pltpu.CompilerParams(vmem_limit_bytes=24 << 20),
    )(*[far(x) for x in scalars], *[near(x) for x in arrays], *[far(x) for x in stored])


def on_device(vectors, previous, diag_tiles, diag_cols, diag_mask, off_tiles, off_rows, off_mask):
    rows, width = vectors.shape
    quarters = lax.axis_size("qtr")
    levels = lax.axis_size("grp").bit_length() - 1
    bits = [1 << 0, 1 << levels // 2, 1 << levels - 1]
    half = ((rows, width), jnp.bfloat16)
    full = ((rows, width), jnp.float32)
    group_half = pltpu.VMEM((quarters * rows, width), jnp.bfloat16)
    group_full = pltpu.VMEM((quarters * rows, width), jnp.float32)

    own = vectors.astype(jnp.bfloat16)
    part2 = swap(own, "qtr", 2)
    arr2 = swap(own, "grp", bits[2])
    part1 = swap(own, "qtr", 1)
    arr1 = swap(own, "grp", bits[1])
    arr0 = swap(own, "grp", bits[0])
    part3 = swap(part2, "qtr", 1)

    keep, send1, send2, send3 = call(
        scatter_kernel, (diag_cols, diag_mask, off_rows, off_mask),
        (off_tiles, own, arr0, arr1, arr2), (full, half, half, half),
        [group_full, pltpu.VMEM(diag_tiles.shape, jnp.bfloat16), pltpu.SemaphoreType.DMA], (diag_tiles,),
    )
    got3 = swap(send3, "qtr", 3)
    got2 = swap(send2, "qtr", 2)
    got1 = swap(send1, "qtr", 1)

    parts = (own, part1, part2, part3)
    away0, away1, away2 = call(
        partner_kernel, (off_rows, off_mask), (off_tiles, *parts),
        (half, half, half), [group_half],
    )
    back2 = swap(away2, "grp", bits[2])
    back1 = swap(away1, "grp", bits[1])
    back0 = swap(away0, "grp", bits[0])
    (base,) = call(
        base_kernel, (diag_cols, diag_mask),
        (diag_tiles, *parts, keep, vectors, previous), (full,), [group_half],
    )

    total = base
    for term in (back0, back1, got1, got3, got2, back2):
        total = total + 2.0 / cheb_half * term.astype(jnp.float32)
    return total


def solution(mesh):
    spread = P(("grp", "qtr"))
    spread_off = P(None, ("grp", "qtr"))
    in_specs = (spread,) * 5 + (spread_off,) * 3
    return jax.shard_map(
        on_device, mesh=mesh, in_specs=in_specs, out_specs=spread, check_vma=False
    )
```

```python
import jax
import jax.numpy as jnp
from jax import lax
from jax.experimental import pallas as pl
from jax.experimental.pallas import tpu as pltpu
from jax.sharding import PartitionSpec as P


cheb_center = 0.25
cheb_half = 2.0


def swap(block, axis, mask):
    count = lax.axis_size(axis)
    return lax.ppermute(block, axis, [(i, i ^ mask) for i in range(count)])


def live(tile, flag):
    return (tile.astype(jnp.float32) * flag.astype(jnp.float32)).astype(jnp.bfloat16)


def dot_plain(a, b):
    return lax.dot_general(a, b, (((1,), (0,)), ((), ())), preferred_element_type=jnp.float32)


def dot_flipped(a, b):
    return lax.dot_general(a, b, (((0,), (0,)), ((), ())), preferred_element_type=jnp.float32)


def spread_add(acc, tiles, flags, places, flipped, block, shift):
    slots, size, _ = tiles.shape
    for slot in range(slots):
        place = pl.multiple_of((places(slot) ^ shift) * size, size)
        tile = live(tiles[slot], flags(slot))
        product = dot_flipped(tile, block) if flipped else dot_plain(tile, block)
        acc[pl.ds(place, size), :] += product


def load_kernel(vectors, *refs):
    staged, sems = refs[-2:]
    count = len(refs) // 2 - 1
    own = refs[count]
    chunks = sems.shape[0] - count
    span = vectors.shape[0] // chunks
    pieces = [pl.ds(i * span, span) for i in range(chunks)]
    copies = [
        pltpu.make_async_copy(vectors.at[rows, :], staged.at[rows, :], sems.at[i])
        for i, rows in enumerate(pieces)
    ]
    copies += [
        pltpu.make_async_copy(refs[i], refs[count + 1 + i], sems.at[chunks + i]) for i in range(count)
    ]
    for copy in copies:
        copy.start()
    for copy, rows in zip(copies, pieces):
        copy.wait()
        own[rows, :] = staged[rows, :].astype(jnp.bfloat16)
    for copy in copies[chunks:]:
        copy.wait()


def partner_spread(acc, partners, arrivals, off_rows, off_mask, off_tiles, shift):
    strips, _, size, _ = off_tiles.shape[1:]
    for partner, arrived in zip(partners, arrivals):
        for strip in range(strips):
            spread_add(
                acc, off_tiles.at[partner, strip], lambda i: off_mask[partner, strip, i],
                lambda i: off_rows[partner, strip, i], False, arrived[strip * size:(strip + 1) * size, :], shift,
            )


def early_kernel(diag_cols, diag_mask, off_rows, off_mask, diag_tiles, off_tiles, own, arr0, arr1, acc):
    strips, _, size, _ = diag_tiles.shape
    shift = strips * lax.axis_index("qtr")
    acc[...] = jnp.zeros_like(acc)
    for strip in range(strips):
        spread_add(
            acc, diag_tiles.at[strip], lambda i: diag_mask[strip, i], lambda i: diag_cols[strip, i],
            True, own[strip * size:(strip + 1) * size, :], shift,
        )
    partner_spread(acc, (0, 1), (arr0, arr1), off_rows, off_mask, off_tiles, shift)


def late_kernel(off_rows, off_mask, off_tiles, arr2, before, acc, out1, out3):
    strips, _, size, _ = off_tiles.shape[1:]
    shift = strips * lax.axis_index("qtr")
    partner_spread(acc, (2,), (arr2,), off_rows, off_mask, off_tiles, shift)
    span = strips * size
    out1[...] = acc[span:2 * span, :].astype(jnp.bfloat16)
    out3[...] = acc[3 * span:, :].astype(jnp.bfloat16)


def collect(parts, gathered):
    span = parts[0].shape[0]
    for i, part in enumerate(parts):
        gathered[i * span:(i + 1) * span, :] = part[...]


def partner_products(partner, out, off_rows, off_mask, off_tiles, gathered, shift):
    strips, slots, size, _ = off_tiles.shape[1:]
    for strip in range(strips):
        total = None
        for slot in range(slots):
            place = pl.multiple_of((off_rows[partner, strip, slot] ^ shift) * size, size)
            tile = live(off_tiles[partner, strip, slot], off_mask[partner, strip, slot])
            term = dot_flipped(tile, gathered[pl.ds(place, size), :])
            total = term if total is None else total + term
        out[strip * size:(strip + 1) * size, :] = total.astype(out.dtype)


def outer_kernel(off_rows, off_mask, off_tiles, part0, part1, part2, part3, gathered, out2, out1):
    shift = off_tiles.shape[1] * lax.axis_index("qtr")
    collect((part0, part1, part2, part3), gathered)
    partner_products(2, out2, off_rows, off_mask, off_tiles, gathered, shift)
    partner_products(1, out1, off_rows, off_mask, off_tiles, gathered, shift)


def inner_kernel(off_rows, off_mask, off_tiles, gathered, out0):
    shift = off_tiles.shape[1] * lax.axis_index("qtr")
    partner_products(0, out0, off_rows, off_mask, off_tiles, gathered, shift)


def base_kernel(diag_cols, diag_mask, diag_tiles, gathered, acc, got1, vectors, previous, base):
    strips, slots, size, _ = diag_tiles.shape
    shift = strips * lax.axis_index("qtr")
    for strip in range(strips):
        rows = pl.ds(strip * size, size)
        total = acc[rows, :] + got1[rows, :].astype(jnp.float32)
        for slot in range(slots):
            place = pl.multiple_of((diag_cols[strip, slot] ^ shift) * size, size)
            tile = live(diag_tiles[strip, slot], diag_mask[strip, slot])
            total = total + dot_plain(tile, gathered[pl.ds(place, size), :])
        base[rows, :] = 2.0 / cheb_half * (total - cheb_center * vectors[rows, :]) - previous[rows, :]


smem = pl.BlockSpec(memory_space=pltpu.SMEM)
vmem = pl.BlockSpec(memory_space=pltpu.VMEM)
anywhere = pl.BlockSpec(memory_space=pl.ANY)


def near(x):
    return pltpu.with_memory_space_constraint(x, pltpu.VMEM)


def far(x):
    return pltpu.with_memory_space_constraint(x, pltpu.HBM)


def call(kernel, scalars, arrays, outs, scratch, stored=(), aliases={}):
    return pl.pallas_call(
        kernel,
        in_specs=[smem] * len(scalars) + [vmem] * len(arrays) + [anywhere] * len(stored),
        out_specs=[vmem] * len(outs),
        out_shape=[pltpu.VMEM(shape, dtype) for shape, dtype in outs],
        scratch_shapes=scratch,
        input_output_aliases=aliases,
        compiler_params=pltpu.CompilerParams(vmem_limit_bytes=24 << 20),
    )(*[near(x) for x in scalars], *[near(x) for x in arrays], *[far(x) for x in stored])


def on_device(vectors, previous, diag_tiles, diag_cols, diag_mask, off_tiles, off_rows, off_mask):
    rows, width = vectors.shape
    quarters = lax.axis_size("qtr")
    levels = lax.axis_size("grp").bit_length() - 1
    bits = [1 << 0, 1 << levels // 2, 1 << levels - 1]
    half = ((rows, width), jnp.bfloat16)
    full = ((rows, width), jnp.float32)
    group_half = ((quarters * rows, width), jnp.bfloat16)
    group_full = ((quarters * rows, width), jnp.float32)

    stored = (diag_tiles, off_tiles, diag_cols, diag_mask, off_rows, off_mask)
    own, diag_tiles, off_tiles, diag_cols, diag_mask, off_rows, off_mask = call(
        load_kernel, (), (), (half, *[(x.shape, x.dtype) for x in stored]),
        [pltpu.VMEM((rows, width), jnp.float32), pltpu.SemaphoreType.DMA((4 + len(stored),))],
        (vectors, *stored),
    )
    part2 = swap(own, "qtr", 2)
    arr2 = swap(own, "grp", bits[2])
    part1 = swap(own, "qtr", 1)
    arr1 = swap(own, "grp", bits[1])
    arr0 = swap(own, "grp", bits[0])
    part3 = swap(part2, "qtr", 1)

    (acc,) = call(
        early_kernel, (diag_cols, diag_mask, off_rows, off_mask),
        (diag_tiles, off_tiles, own, arr0, arr1), (group_full,), [],
    )
    acc, send1, send3 = call(
        late_kernel, (off_rows, off_mask), (off_tiles, arr2, acc),
        (group_full, half, half), [], aliases={4: 0},
    )
    got3 = swap(send3, "qtr", 1)
    send2 = (acc[2 * rows:3 * rows] + got3.astype(jnp.float32)).astype(jnp.bfloat16)
    got2 = swap(send2, "qtr", 2)
    got1 = swap(send1, "qtr", 1)

    parts = (own, part1, part2, part3)
    gathered, away2, away1 = call(
        outer_kernel, (off_rows, off_mask), (off_tiles, *parts),
        (group_half, half, half), [],
    )
    back2 = swap(away2, "grp", bits[2])
    back1 = swap(away1, "grp", bits[1])
    (away0,) = call(inner_kernel, (off_rows, off_mask), (off_tiles, gathered), (half,), [])
    back0 = swap(away0, "grp", bits[0])
    (base,) = call(
        base_kernel, (diag_cols, diag_mask),
        (diag_tiles, gathered, acc, got1, vectors, previous), (full,), [],
    )

    total = base
    for term in (back0, back1, got2, back2):
        total = total + 2.0 / cheb_half * term.astype(jnp.float32)
    return total


def solution(mesh):
    spread = P(("grp", "qtr"))
    spread_off = P(None, ("grp", "qtr"))
    in_specs = (spread,) * 5 + (spread_off,) * 3
    return jax.shard_map(
        on_device, mesh=mesh, in_specs=in_specs, out_specs=spread, check_vma=False
    )
```

```python
import jax
import jax.numpy as jnp
from jax import lax
from jax.experimental import pallas as pl
from jax.experimental.pallas import tpu as pltpu
from jax.sharding import PartitionSpec as P


cheb_center = 0.25
cheb_half = 2.0


def swap(block, axis, mask):
    count = lax.axis_size(axis)
    return lax.ppermute(block, axis, [(i, i ^ mask) for i in range(count)])


def live(tile, flag):
    return (tile.astype(jnp.float32) * flag.astype(jnp.float32)).astype(jnp.bfloat16)


def dot_plain(a, b):
    return lax.dot_general(a, b, (((1,), (0,)), ((), ())), preferred_element_type=jnp.float32)


def dot_flipped(a, b):
    return lax.dot_general(a, b, (((0,), (0,)), ((), ())), preferred_element_type=jnp.float32)


def spread_add(acc, tiles, flags, places, flipped, block, shift):
    slots, size, _ = tiles.shape
    for slot in range(slots):
        place = pl.multiple_of((places(slot) ^ shift) * size, size)
        tile = live(tiles[slot], flags(slot))
        product = dot_flipped(tile, block) if flipped else dot_plain(tile, block)
        acc[pl.ds(place, size), :] += product


def load_kernel(vectors, *refs):
    staged, sems = refs[-2:]
    count = len(refs) // 2 - 1
    own = refs[count]
    chunks = sems.shape[0] - count
    span = vectors.shape[0] // chunks
    pieces = [pl.ds(i * span, span) for i in range(chunks)]
    copies = [
        pltpu.make_async_copy(vectors.at[rows, :], staged.at[rows, :], sems.at[i])
        for i, rows in enumerate(pieces)
    ]
    copies += [
        pltpu.make_async_copy(refs[i], refs[count + 1 + i], sems.at[chunks + i]) for i in range(count)
    ]
    for copy in copies:
        copy.start()
    for copy, rows in zip(copies, pieces):
        copy.wait()
        own[rows, :] = staged[rows, :].astype(jnp.bfloat16)
    for copy in copies[chunks:]:
        copy.wait()


def partner_spread(acc, partners, arrivals, off_rows, off_mask, off_tiles, shift):
    strips, _, size, _ = off_tiles.shape[1:]
    for partner, arrived in zip(partners, arrivals):
        for strip in range(strips):
            spread_add(
                acc, off_tiles.at[partner, strip], lambda i: off_mask[partner, strip, i],
                lambda i: off_rows[partner, strip, i], False, arrived[strip * size:(strip + 1) * size, :], shift,
            )


def scatter_kernel(
    diag_cols, diag_mask, off_rows, off_mask, diag_tiles, off_tiles, own, arr0, arr1, arr2, acc, out1, out3,
):
    strips, _, size, _ = diag_tiles.shape
    shift = strips * lax.axis_index("qtr")
    acc[...] = jnp.zeros_like(acc)
    for strip in range(strips):
        spread_add(
            acc, diag_tiles.at[strip], lambda i: diag_mask[strip, i], lambda i: diag_cols[strip, i],
            True, own[strip * size:(strip + 1) * size, :], shift,
        )
    partner_spread(acc, (0, 1, 2), (arr0, arr1, arr2), off_rows, off_mask, off_tiles, shift)
    span = strips * size
    out1[...] = acc[span:2 * span, :].astype(jnp.bfloat16)
    out3[...] = acc[3 * span:, :].astype(jnp.bfloat16)


def partner_products(partner, out, off_rows, off_mask, off_tiles, gathered, shift):
    strips, slots, size, _ = off_tiles.shape[1:]
    for strip in range(strips):
        tiles, blocks = [], []
        for slot in range(slots):
            place = pl.multiple_of((off_rows[partner, strip, slot] ^ shift) * size, size)
            tiles.append(live(off_tiles[partner, strip, slot], off_mask[partner, strip, slot]))
            blocks.append(gathered[pl.ds(place, size), :])
        total = dot_flipped(jnp.concatenate(tiles, 0), jnp.concatenate(blocks, 0))
        out[strip * size:(strip + 1) * size, :] = total.astype(out.dtype)


def partner_kernel(off_rows, off_mask, off_tiles, part0, part1, part2, part3, gathered, out2, out1, out0):
    span = part0.shape[0]
    shift = off_tiles.shape[1] * lax.axis_index("qtr")
    for i, part in enumerate((part0, part1, part2, part3)):
        gathered[i * span:(i + 1) * span, :] = part[...]
    for partner, out in ((2, out2), (1, out1), (0, out0)):
        partner_products(partner, out, off_rows, off_mask, off_tiles, gathered, shift)


def base_kernel(diag_cols, diag_mask, diag_tiles, gathered, acc, got1, vectors, previous, base):
    strips, slots, size, _ = diag_tiles.shape
    shift = strips * lax.axis_index("qtr")
    for strip in range(strips):
        rows = pl.ds(strip * size, size)
        total = acc[rows, :] + got1[rows, :].astype(jnp.float32)
        for slot in range(slots):
            place = pl.multiple_of((diag_cols[strip, slot] ^ shift) * size, size)
            tile = live(diag_tiles[strip, slot], diag_mask[strip, slot])
            total = total + dot_plain(tile, gathered[pl.ds(place, size), :])
        base[rows, :] = 2.0 / cheb_half * (total - cheb_center * vectors[rows, :]) - previous[rows, :]


smem = pl.BlockSpec(memory_space=pltpu.SMEM)
vmem = pl.BlockSpec(memory_space=pltpu.VMEM)
anywhere = pl.BlockSpec(memory_space=pl.ANY)


def near(x):
    return pltpu.with_memory_space_constraint(x, pltpu.VMEM)


def far(x):
    return pltpu.with_memory_space_constraint(x, pltpu.HBM)


def call(kernel, scalars, arrays, outs, scratch, stored=(), aliases={}):
    return pl.pallas_call(
        kernel,
        in_specs=[smem] * len(scalars) + [vmem] * len(arrays) + [anywhere] * len(stored),
        out_specs=[vmem] * len(outs),
        out_shape=[pltpu.VMEM(shape, dtype) for shape, dtype in outs],
        scratch_shapes=scratch,
        input_output_aliases=aliases,
        compiler_params=pltpu.CompilerParams(vmem_limit_bytes=24 << 20),
    )(*[near(x) for x in scalars], *[near(x) for x in arrays], *[far(x) for x in stored])


def on_device(vectors, previous, diag_tiles, diag_cols, diag_mask, off_tiles, off_rows, off_mask):
    rows, width = vectors.shape
    quarters = lax.axis_size("qtr")
    levels = lax.axis_size("grp").bit_length() - 1
    bits = [1 << 0, 1 << levels // 2, 1 << levels - 1]
    half = ((rows, width), jnp.bfloat16)
    full = ((rows, width), jnp.float32)
    group_half = ((quarters * rows, width), jnp.bfloat16)
    group_full = ((quarters * rows, width), jnp.float32)

    stored = (diag_tiles, diag_cols, diag_mask, off_rows, off_mask)
    own, diag_tiles, diag_cols, diag_mask, off_rows, off_mask = call(
        load_kernel, (), (), (half, *[(x.shape, x.dtype) for x in stored]),
        [pltpu.VMEM((rows, width), jnp.float32), pltpu.SemaphoreType.DMA((4 + len(stored),))],
        (vectors, *stored),
    )
    part2 = swap(own, "qtr", 2)
    arr2 = swap(own, "grp", bits[2])
    part1 = swap(own, "qtr", 1)
    arr1 = swap(own, "grp", bits[1])
    arr0 = swap(own, "grp", bits[0])
    part3 = swap(part2, "qtr", 1)

    acc, send1, send3 = call(
        scatter_kernel, (diag_cols, diag_mask, off_rows, off_mask),
        (diag_tiles, off_tiles, own, arr0, arr1, arr2), (group_full, half, half), [],
    )
    got3 = swap(send3, "qtr", 1)
    send2 = (acc[2 * rows:3 * rows] + got3.astype(jnp.float32)).astype(jnp.bfloat16)
    got2 = swap(send2, "qtr", 2)
    got1 = swap(send1, "qtr", 1)

    parts = (own, part1, part2, part3)
    gathered, away2, away1, away0 = call(
        partner_kernel, (off_rows, off_mask), (off_tiles, *parts),
        (group_half, half, half, half), [],
    )
    back2 = swap(away2, "grp", bits[2])
    back1 = swap(away1, "grp", bits[1])
    back0 = swap(away0, "grp", bits[0])
    (base,) = call(
        base_kernel, (diag_cols, diag_mask),
        (diag_tiles, gathered, acc, got1, vectors, previous), (full,), [],
    )

    total = base
    for term in (back0, back1, got2, back2):
        total = total + 2.0 / cheb_half * term.astype(jnp.float32)
    return total


def solution(mesh):
    spread = P(("grp", "qtr"))
    spread_off = P(None, ("grp", "qtr"))
    in_specs = (spread,) * 5 + (spread_off,) * 3
    return jax.shard_map(
        on_device, mesh=mesh, in_specs=in_specs, out_specs=spread, check_vma=False
    )
```

```python
import jax
import jax.numpy as jnp
from jax import lax
from jax.experimental import pallas as pl
from jax.experimental.pallas import tpu as pltpu
from jax.sharding import PartitionSpec as P


cheb_center = 0.25
cheb_half = 2.0


def swap(block, axis, mask):
    count = lax.axis_size(axis)
    return lax.ppermute(block, axis, [(i, i ^ mask) for i in range(count)])


def live(tile, flag):
    return (tile.astype(jnp.float32) * flag.astype(jnp.float32)).astype(jnp.bfloat16)


def dot_plain(a, b):
    return lax.dot_general(a, b, (((1,), (0,)), ((), ())), preferred_element_type=jnp.float32)


def dot_flipped(a, b):
    return lax.dot_general(a, b, (((0,), (0,)), ((), ())), preferred_element_type=jnp.float32)


def spread_add(acc, tiles, flags, places, flipped, block, shift):
    slots, size, _ = tiles.shape
    for slot in range(slots):
        place = pl.multiple_of((places(slot) ^ shift) * size, size)
        tile = live(tiles[slot], flags(slot))
        product = dot_flipped(tile, block) if flipped else dot_plain(tile, block)
        acc[pl.ds(place, size), :] += product


def load_kernel(vectors, *refs):
    staged, sems = refs[-2:]
    count = len(refs) // 2 - 1
    own = refs[count]
    chunks = sems.shape[0] - count
    span = vectors.shape[0] // chunks
    pieces = [pl.ds(i * span, span) for i in range(chunks)]
    copies = [
        pltpu.make_async_copy(vectors.at[rows, :], staged.at[rows, :], sems.at[i])
        for i, rows in enumerate(pieces)
    ]
    copies += [
        pltpu.make_async_copy(refs[i], refs[count + 1 + i], sems.at[chunks + i]) for i in range(count)
    ]
    for copy in copies:
        copy.start()
    for copy, rows in zip(copies, pieces):
        copy.wait()
        own[rows, :] = staged[rows, :].astype(jnp.bfloat16)
    for copy in copies[chunks:]:
        copy.wait()


def partner_spread(acc, partners, arrivals, off_rows, off_mask, off_tiles, shift):
    strips, _, size, _ = off_tiles.shape[1:]
    for partner, arrived in zip(partners, arrivals):
        for strip in range(strips):
            spread_add(
                acc, off_tiles.at[partner, strip], lambda i: off_mask[partner, strip, i],
                lambda i: off_rows[partner, strip, i], False, arrived[strip * size:(strip + 1) * size, :], shift,
            )


def scatter_kernel(
    diag_cols, diag_mask, off_rows, off_mask, diag_tiles, off_tiles, own, arr0, arr1, arr2, acc, out1, out3,
):
    strips, _, size, _ = diag_tiles.shape
    shift = strips * lax.axis_index("qtr")
    acc[...] = jnp.zeros_like(acc)
    for strip in range(strips):
        spread_add(
            acc, diag_tiles.at[strip], lambda i: diag_mask[strip, i], lambda i: diag_cols[strip, i],
            True, own[strip * size:(strip + 1) * size, :], shift,
        )
    partner_spread(acc, (0, 1, 2), (arr0, arr1, arr2), off_rows, off_mask, off_tiles, shift)
    span = strips * size
    out1[...] = acc[span:2 * span, :].astype(jnp.bfloat16)
    out3[...] = acc[3 * span:, :].astype(jnp.bfloat16)


def partner_products(partner, out, off_rows, off_mask, off_tiles, gathered, shift):
    strips, slots, size, _ = off_tiles.shape[1:]
    for strip in range(strips):
        tiles, blocks = [], []
        for slot in range(slots):
            place = pl.multiple_of((off_rows[partner, strip, slot] ^ shift) * size, size)
            tiles.append(live(off_tiles[partner, strip, slot], off_mask[partner, strip, slot]))
            blocks.append(gathered[pl.ds(place, size), :])
        total = dot_flipped(jnp.concatenate(tiles, 0), jnp.concatenate(blocks, 0))
        out[strip * size:(strip + 1) * size, :] = total.astype(out.dtype)


def partner_kernel(off_rows, off_mask, off_tiles, part0, part1, part2, part3, gathered, out2, out1, out0):
    span = part0.shape[0]
    shift = off_tiles.shape[1] * lax.axis_index("qtr")
    for i, part in enumerate((part0, part1, part2, part3)):
        gathered[i * span:(i + 1) * span, :] = part[...]
    for partner, out in ((2, out2), (1, out1), (0, out0)):
        partner_products(partner, out, off_rows, off_mask, off_tiles, gathered, shift)


def base_kernel(diag_cols, diag_mask, diag_tiles, gathered, acc, got1, vectors, previous, base):
    strips, slots, size, _ = diag_tiles.shape
    shift = strips * lax.axis_index("qtr")
    for strip in range(strips):
        rows = pl.ds(strip * size, size)
        total = acc[rows, :] + got1[rows, :].astype(jnp.float32)
        tiles, blocks = [], []
        for slot in range(slots):
            place = pl.multiple_of((diag_cols[strip, slot] ^ shift) * size, size)
            tiles.append(live(diag_tiles[strip, slot], diag_mask[strip, slot]))
            blocks.append(gathered[pl.ds(place, size), :])
        total = total + dot_plain(jnp.concatenate(tiles, 1), jnp.concatenate(blocks, 0))
        base[rows, :] = 2.0 / cheb_half * (total - cheb_center * vectors[rows, :]) - previous[rows, :]


smem = pl.BlockSpec(memory_space=pltpu.SMEM)
vmem = pl.BlockSpec(memory_space=pltpu.VMEM)
anywhere = pl.BlockSpec(memory_space=pl.ANY)


def near(x):
    return pltpu.with_memory_space_constraint(x, pltpu.VMEM)


def far(x):
    return pltpu.with_memory_space_constraint(x, pltpu.HBM)


def call(kernel, scalars, arrays, outs, scratch, stored=(), aliases={}):
    return pl.pallas_call(
        kernel,
        in_specs=[smem] * len(scalars) + [vmem] * len(arrays) + [anywhere] * len(stored),
        out_specs=[vmem] * len(outs),
        out_shape=[pltpu.VMEM(shape, dtype) for shape, dtype in outs],
        scratch_shapes=scratch,
        input_output_aliases=aliases,
        compiler_params=pltpu.CompilerParams(vmem_limit_bytes=24 << 20),
    )(*[near(x) for x in scalars], *[near(x) for x in arrays], *[far(x) for x in stored])


def on_device(vectors, previous, diag_tiles, diag_cols, diag_mask, off_tiles, off_rows, off_mask):
    rows, width = vectors.shape
    quarters = lax.axis_size("qtr")
    levels = lax.axis_size("grp").bit_length() - 1
    bits = [1 << 0, 1 << levels // 2, 1 << levels - 1]
    half = ((rows, width), jnp.bfloat16)
    full = ((rows, width), jnp.float32)
    group_half = ((quarters * rows, width), jnp.bfloat16)
    group_full = ((quarters * rows, width), jnp.float32)

    stored = (diag_tiles, diag_cols, diag_mask, off_rows, off_mask)
    own, diag_tiles, diag_cols, diag_mask, off_rows, off_mask = call(
        load_kernel, (), (), (half, *[(x.shape, x.dtype) for x in stored]),
        [pltpu.VMEM((rows, width), jnp.float32), pltpu.SemaphoreType.DMA((4 + len(stored),))],
        (vectors, *stored),
    )
    part2 = swap(own, "qtr", 2)
    arr2 = swap(own, "grp", bits[2])
    part1 = swap(own, "qtr", 1)
    arr1 = swap(own, "grp", bits[1])
    arr0 = swap(own, "grp", bits[0])
    part3 = swap(part2, "qtr", 1)

    acc, send1, send3 = call(
        scatter_kernel, (diag_cols, diag_mask, off_rows, off_mask),
        (diag_tiles, off_tiles, own, arr0, arr1, arr2), (group_full, half, half), [],
    )
    got3 = swap(send3, "qtr", 1)
    send2 = (acc[2 * rows:3 * rows] + got3.astype(jnp.float32)).astype(jnp.bfloat16)
    got2 = swap(send2, "qtr", 2)
    got1 = swap(send1, "qtr", 1)

    parts = (own, part1, part2, part3)
    gathered, away2, away1, away0 = call(
        partner_kernel, (off_rows, off_mask), (off_tiles, *parts),
        (group_half, half, half, half), [],
    )
    back2 = swap(away2, "grp", bits[2])
    back1 = swap(away1, "grp", bits[1])
    back0 = swap(away0, "grp", bits[0])
    (base,) = call(
        base_kernel, (diag_cols, diag_mask),
        (diag_tiles, gathered, acc, got1, vectors, previous), (full,), [],
    )

    total = base
    for term in (back0, back1, got2, back2):
        total = total + 2.0 / cheb_half * term.astype(jnp.float32)
    return total


def solution(mesh):
    spread = P(("grp", "qtr"))
    spread_off = P(None, ("grp", "qtr"))
    in_specs = (spread,) * 5 + (spread_off,) * 3
    return jax.shard_map(
        on_device, mesh=mesh, in_specs=in_specs, out_specs=spread, check_vma=False
    )
```
